32 devices in a mesh: freq: 4 (over z), space: 8 (over y, x, core).
Axes of the slice: x: 2, y: 2, z: 4, core: 2. Of those that a mesh axis runs over, the one named last changes fastest.
Arguments:
- recorded: bfloat16 [8, 2, 2048, 128], P('freq', None, 'space'), may hold values from -6 to 6
- v_factors: bfloat16 [8, 8, 2, 2048, 128], P('freq', None, None, 'space'), may hold values from -0.25 to 0.25
- u_factors: bfloat16 [8, 2, 2048, 8, 128], P('freq', None, 'space'), may hold values from -0.25 to 0.25
- tile_ranks: int32 [8, 8, 8], P('freq'), may hold values from 0 to 128, as said below
- mute_start: int32 [2048, 128], P('space', 'freq'), may hold values from 0 to 127
Outputs:
- muted_traces: float32 [2048, 128, 128], P('space', 'freq')
The draws below stay inside these ranges and needn't reach their ends.
Inputs may be any that keep to these rules, and one draw needn't show every extreme that they name: `tile_ranks`: entries with i equal to j are 128; every other entry is 0 or 64.
All inputs are finite; a program needn't handle non-finite values.
Results may differ from the reference program's by a relative error of at most 0.0041.
Values may be sent and summed in bfloat16 or wider, within the bound.
A program may use at most 64 MiB of HBM per device.

```python
import math
import jax
import jax.numpy as jnp
from jax import lax

TILE = 256
RMAX = 128
NS = 128
NT = 128
F = 8
NTILE = 8
NR = 2048


def draw_tile_ranks(key, part):
    tile_count = NR // TILE
    rolled_values = jax.random.randint(key, (F, tile_count, tile_count), 0, 9)
    levels = jnp.where(rolled_values < 4, RMAX // 2, 0)
    lines = jnp.arange(tile_count, dtype=jnp.int32)
    diagonal = (lines[:, None] == lines[None, :])[None, :, :]
    return jnp.where(diagonal, RMAX, levels).astype(jnp.int32)


def with_ends(entries, rng, smallest, largest):
    longest = entries.shape.index(max(entries.shape))
    spots = []
    for shift in (0, 1):
        where = [jax.random.randint(jax.random.fold_in(rng, axis), (), 0, length) for axis, length in enumerate(entries.shape)]
        where[longest] = (where[longest] + shift) % entries.shape[longest]
        spots.append(tuple(where))
    return entries.at[spots[0]].set(smallest).at[spots[1]].set(largest)


def shard_levels(own_key, shape, shards, low, top_value):
    loudness = 1.0
    for position, parts in shards:
        steps = jax.random.uniform(jax.random.fold_in(jax.random.fold_in(own_key, 6), position), (parts,), jnp.float32, low / len(shards), top_value / len(shards))
        loudness = loudness * jnp.repeat(jnp.exp(steps), shape[position] // parts).reshape((-1,) + (1,) * (len(shape) - 1 - position))
    return loudness


def gaussian(rng, dims, scale, limit, cuts=(), kind=jnp.bfloat16):
    drawn = jax.random.normal(rng, dims, jnp.float32) * scale
    if len(cuts) > 0:
        drawn = shard_levels(rng, dims, cuts, -0.22, 0.18) * drawn
    return jnp.clip(drawn, min=-limit, max=limit).astype(kind)


def setup_inputs(seed: int = 0) -> dict:
    key_list = jax.random.split(jax.random.key(seed), 6)
    return {
        "recorded": gaussian(key_list[0], (F, 2, NR, NS), 1.0, 6.0, ((0, 4), (2, 8))),
        "v_factors": gaussian(key_list[1], (F, NTILE, 2, NR, RMAX), (2 * TILE) ** -0.5, 0.25, ((0, 4), (3, 8))),
        "u_factors": gaussian(key_list[2], (F, 2, NR, NTILE, RMAX), (2 * (RMAX + (NTILE - 1) * RMAX * 2 // 9)) ** -0.5, 0.25, ((0, 4), (2, 8))),
        "tile_ranks": draw_tile_ranks(jax.random.fold_in(key_list[5], 71), 0),
        "mute_start": with_ends(jax.random.randint(key_list[4], (NR, NS), 0, NT), jax.random.fold_in(key_list[4], 1), 0, NT - 1).astype(jnp.int32),
    }


def reference(recorded, v_factors, u_factors, tile_ranks, mute_start):
    tile_count = NR // TILE
    spectra_list = []
    for slot in range(F):
        data_freq = recorded[slot].astype(jnp.float32).reshape(2, tile_count, TILE, NS)
        v_freq = v_factors[slot].reshape(tile_count, 2, tile_count, TILE, RMAX)
        u_freq = jnp.moveaxis(u_factors[slot].reshape(2, tile_count, TILE, tile_count, RMAX), 1, 0)

        def one_row(row_items):
            v_row, u_row, rank_row = row_items
            v_row = v_row.astype(jnp.float32)
            u_row = u_row.astype(jnp.float32)
            high = lax.Precision.HIGHEST
            block_real = jnp.einsum('jqk,jqs->jks', v_row[0], data_freq[0], precision=high) - jnp.einsum('jqk,jqs->jks', v_row[1], data_freq[1], precision=high)
            block_imag = jnp.einsum('jqk,jqs->jks', v_row[0], data_freq[1], precision=high) + jnp.einsum('jqk,jqs->jks', v_row[1], data_freq[0], precision=high)
            kept = (jnp.arange(RMAX, dtype=jnp.int32)[None, :] < rank_row[:, None])[:, :, None]
            block_real = lax.optimization_barrier(jnp.where(kept, block_real, 0.0).astype(jnp.bfloat16)).astype(jnp.float32)
            block_imag = lax.optimization_barrier(jnp.where(kept, block_imag, 0.0).astype(jnp.bfloat16)).astype(jnp.float32)
            real_part = jnp.einsum('pjk,jks->ps', u_row[0], block_real, precision=high) - jnp.einsum('pjk,jks->ps', u_row[1], block_imag, precision=high)
            imag_part = jnp.einsum('pjk,jks->ps', u_row[0], block_imag, precision=high) + jnp.einsum('pjk,jks->ps', u_row[1], block_real, precision=high)
            return jnp.stack([real_part, imag_part]).astype(jnp.bfloat16)
        row_spectra = lax.map(one_row, (v_freq, u_freq, tile_ranks[slot]))
        spectra_list.append(jnp.moveaxis(row_spectra, 1, 0).reshape(2, NR, NS))
    spectra = lax.optimization_barrier(jnp.stack(spectra_list)).astype(jnp.float32)
    freq_index = jnp.arange(F, dtype=jnp.int32)
    weights = 1 + freq_index * (NT // 2 // F)
    times = jnp.arange(NT, dtype=jnp.int32)
    phase = (weights[:, None] * times[None, :] % NT).astype(jnp.float32) * (2.0 * math.pi / NT)
    scale = 1.0 / math.sqrt(2.0 * F)
    cos_basis = jnp.cos(phase) * scale
    sin_basis = -jnp.sin(phase) * scale
    high = lax.Precision.HIGHEST
    traces = jnp.einsum('fps,ft->pst', spectra[:, 0], cos_basis, precision=high) + jnp.einsum('fps,ft->pst', spectra[:, 1], sin_basis, precision=high)
    return jnp.where(times[None, None, :] >= mute_start[:, :, None], traces, 0.0)
```

```python
import functools
import math

import jax
import jax.numpy as jnp
import ml_dtypes
import numpy as np
from jax import lax
from jax.experimental import pallas as pl
from jax.experimental.pallas import tpu as pltpu
from jax.sharding import PartitionSpec as P

NT = 128
GROUP = 8
NT_DIMS = (((1,), (1,)), ((), ()))


def flipped(index, mask):
    result = index
    bit = 1
    while bit <= mask:
        if mask & bit:
            result = result + bit * (1 - 2 * ((index // bit) % 2))
        bit *= 2
    return result


def nth_target(step, me_z, parts):
    if step == parts - 1:
        return me_z
    return step + (step - me_z + parts) // parts


def spectra_kernel(
    tiles, parts, ranks_hbm, recorded_hbm, v_hbm, u_hbm, mute_hbm, out_ref, mask_ref,
    ranks_ref, recorded_ref, mute_ref, v_ref, u_ref, wide_ref, data_ref, send_ref, recv_ref, factor_ref, spec_ref,
    v_sems, u_sems, send_sems, recv_sems, zsend_sems, zrecv_sems, first_sems,
):
    me = lax.axis_index("space")
    me_z = lax.axis_index("freq")
    freqs = recorded_ref.shape[0]
    tile = recorded_ref.shape[2]
    sources = recorded_ref.shape[3]
    ranks = v_ref.shape[3]
    half = ranks // 2
    share = sources // parts
    rows = tile // parts
    order = list(range(tiles - 1, -1, -1))

    v_copies = [
        pltpu.make_async_copy(v_hbm.at[f], v_ref.at[f], v_sems.at[f]) for f in range(freqs)
    ]
    u_copies = [
        pltpu.make_async_copy(u_hbm.at[f], u_ref.at[f], u_sems.at[f]) for f in range(freqs)
    ]
    ranks_copy = pltpu.make_async_copy(ranks_hbm, ranks_ref, first_sems.at[0])
    data_copy = pltpu.make_async_copy(recorded_hbm, recorded_ref, first_sems.at[1])
    mute_copy = pltpu.make_async_copy(mute_hbm, mute_ref, first_sems.at[2])
    data_copy.start()
    ranks_copy.start()
    for copy in v_copies + u_copies:
        copy.start()
    mute_copy.start()

    barrier = pltpu.get_barrier_semaphore()
    for r in range(1, tiles):
        pl.semaphore_signal(
            barrier, inc=1, device_id={"space": flipped(me, r)}, device_id_type=pl.DeviceIdType.MESH
        )
    for r in range(1, parts):
        pl.semaphore_signal(
            barrier, inc=1, device_id={"freq": flipped(me_z, r)},
            device_id_type=pl.DeviceIdType.MESH,
        )

    def space_copy(f, n, r):
        return pltpu.make_async_remote_copy(
            src_ref=send_ref.at[f, n, r],
            dst_ref=recv_ref.at[f, n, r],
            send_sem=send_sems.at[f, n],
            recv_sem=recv_sems.at[f, n],
            device_id={"space": flipped(me, r)},
            device_id_type=pl.DeviceIdType.MESH,
        )

    def arrivals(ref, sem):
        return pltpu.make_async_copy(ref.at[pl.ds(1, tiles - 1)], ref.at[pl.ds(1, tiles - 1)], sem)

    def send_step(f, n):
        for r in order[:-1]:
            space_copy(f, n, r).start()

    def freq_copy(f, n):
        return pltpu.make_async_remote_copy(
            src_ref=spec_ref.at[f, n],
            dst_ref=out_ref.at[me_z, f],
            send_sem=zsend_sems.at[f, n],
            recv_sem=zrecv_sems.at[f, me_z],
            device_id={"freq": nth_target(n, me_z, parts)},
            device_id_type=pl.DeviceIdType.MESH,
        )

    lane = lax.broadcasted_iota(jnp.int32, (share, ranks), 1)
    low = lane < half
    rank_of = lax.rem(lane, half)
    data_copy.wait()
    for f in range(freqs):
        real = recorded_ref[f, 0].astype(jnp.float32).T.astype(jnp.bfloat16)
        imag = recorded_ref[f, 1].astype(jnp.float32).T.astype(jnp.bfloat16)
        for z in range(parts):
            part = slice(z * share, (z + 1) * share)
            data_ref[f, z, :share, :tile] = real[part]
            data_ref[f, z, :share, tile:] = -imag[part]
            data_ref[f, z, share:, :tile] = -imag[part]
            data_ref[f, z, share:, tile:] = -real[part]
    ranks_copy.wait()

    def first_stage(f):
        v_copies[f].wait()
        lhs = jnp.concatenate([data_ref[f, nth_target(n, me_z, parts)] for n in range(parts)], axis=0)
        for first in range(0, tiles, 2):
            group = order[first : first + 2]
            targets = [flipped(me, r) for r in group]
            pair = jnp.concatenate([v_ref[f, row] for row in targets], axis=1)
            blocks = jnp.dot(lhs, pair, preferred_element_type=jnp.float32)
            for t, (r, row) in enumerate(zip(group, targets)):
                columns = slice(t * ranks, (t + 1) * ranks)
                limit = ranks_ref[f, row, me]
                keep = rank_of < limit
                for n in range(parts):
                    at = n * 2 * share
                    real, imag = blocks[at : at + share, columns], blocks[at + share : at + 2 * share, columns]
                    packed = jnp.where(low, real, pltpu.roll(imag, half, 1))
                    packed = jnp.where(keep, packed, 0.0).astype(jnp.bfloat16)
                    if r == 0:
                        recv_ref[f, n, 0] = packed
                        packed = jnp.where(low, pltpu.roll(real, half, 1), imag)
                        kept = rank_of + half < limit
                        recv_ref[f, n, tiles] = jnp.where(kept, packed, 0.0).astype(jnp.bfloat16)
                    else:
                        send_ref[f, n, r] = packed

    for f in range(freqs):
        first_stage(f)
        if f == 0:
            pl.semaphore_wait(barrier, tiles - 1 + parts - 1)
        send_step(f, 0)
    for n in range(1, parts):
        for f in range(freqs):
            send_step(f, n)

    wide_low = lax.broadcasted_iota(jnp.int32, (tile, ranks), 1) < half

    def prepare(f):
        u_copies[f].wait()
        for c in range(2):
            wide_ref[c] = u_ref[f, c].astype(jnp.float32)
        for r in range(tiles):
            start = flipped(me, r)
            real = wide_ref[0, pl.ds(start, tile, stride=tiles), :]
            imag = wide_ref[1, pl.ds(start, tile, stride=tiles), :]
            packed = jnp.where(wide_low, real, pltpu.roll(imag, half, 1))
            factor_ref[f, :, r * ranks : (r + 1) * ranks] = packed.astype(jnp.bfloat16)
            if r == 0:
                packed = jnp.where(wide_low, pltpu.roll(real, half, 1), imag)
                factor_ref[f, :, tiles * ranks :] = packed.astype(jnp.bfloat16)

    for f in range(freqs):
        prepare(f)

    swap_lane = lax.broadcasted_iota(jnp.int32, (rows, sources), 1)
    for n in range(parts):
        for f in range(freqs):
            arrivals(recv_ref.at[f, n], recv_sems.at[f, n]).wait()
            plain, turned = [], []
            for r in range(tiles + 1):
                block = recv_ref[f, n, r]
                plain.append(block)
                swapped = pltpu.roll(block.astype(jnp.float32), half, 1)
                turned.append(jnp.where(low, -swapped, swapped).astype(jnp.bfloat16))
            rhs = jnp.concatenate(
                [jnp.concatenate(plain, axis=1), jnp.concatenate(turned, axis=1)], axis=0
            )
            total = lax.dot_general(factor_ref[f], rhs, NT_DIMS, preferred_element_type=jnp.float32)
            if total.shape[1] < sources:
                total = jnp.concatenate([total, total], axis=1)
            for c in range(2):
                merged = None
                for q in range(parts):
                    piece = total[q * rows : (q + 1) * rows]
                    shift = (q - c) * share % sources
                    if shift:
                        piece = pltpu.roll(piece, shift, 1)
                    merged = piece if q == 0 else jnp.where(swap_lane < q * share, merged, piece)
                merged = merged.astype(jnp.bfloat16)
                if n == parts - 1:
                    out_ref[me_z, f, c * rows : (c + 1) * rows] = merged
                else:
                    spec_ref[f, n, c * rows : (c + 1) * rows] = merged
            if n < parts - 1:
                freq_copy(f, n).start()

    mute_copy.wait()
    times = lax.broadcasted_iota(jnp.int32, (share, NT), 1)
    span = 2 * GROUP
    for n in range(rows // span):
      for q in range(parts):
          for i in range(span):
              p = q * rows + n * span + i
              at = (q * span + i) * share
              starts = mute_ref[:, p : p + 1]
              mask_ref[n, at : at + share] = jnp.where(times >= starts, 1.0, 0.0).astype(jnp.bfloat16)

    for n in range(parts):
        for f in range(freqs):
            arrivals(send_ref.at[f, n], send_sems.at[f, n]).wait()
    for n in range(parts - 1):
        for f in range(freqs):
            freq_copy(f, n).wait_send()
    for r in range(1, parts):
        for f in range(freqs):
            source = flipped(me_z, r)
            pltpu.make_async_copy(
                out_ref.at[source, f], out_ref.at[source, f], zrecv_sems.at[f, source]
            ).wait()


def time_kernel(
    share, spec_ref, mask_ref, basis_ref, out_hbm, rows_ref, out_sems,
):
    parts, freqs, rows, sources = spec_ref.shape
    rows //= 2
    copies = []
    for n in range(rows // (2 * GROUP)):
        sides = []
        for g in (2 * n, 2 * n + 1):
            pieces = []
            for z in range(parts):
                for f in range(freqs):
                    for c in range(2):
                        at = c * rows + g * GROUP
                        pieces.append(spec_ref[z, f, at : at + GROUP].astype(jnp.float32))
            block = jnp.concatenate(pieces, axis=0)
            sides.append(block.T.astype(jnp.bfloat16))
        lhs = jnp.concatenate(sides, axis=0)
        lhs = jnp.concatenate([lhs, lhs], axis=1)
        for pair in range(GROUP // 2):
            product = jnp.dot(
                lhs, basis_ref[:, pair * 2 * NT : (pair + 1) * 2 * NT], preferred_element_type=jnp.float32
            )
            for side in range(2):
                for q in range(parts):
                    for e in range(2):
                        p = q * rows + (2 * n + side) * GROUP + pair * 2 + e
                        at = side * sources + q * share
                        values = product[at : at + share, e * NT : (e + 1) * NT]
                        row = (q * 2 * GROUP + side * GROUP + pair * 2 + e) * share
                        mask = mask_ref[n, row : row + share].astype(jnp.float32)
                        rows_ref[p * share : (p + 1) * share, :] = values * mask
        for q in range(parts):
            span = pl.ds((q * rows + 2 * n * GROUP) * share, 2 * GROUP * share)
            copy = pltpu.make_async_copy(rows_ref.at[span], out_hbm.at[span], out_sems.at[n, q])
            copy.start()
            copies.append(copy)
    for copy in copies:
        copy.wait()


def block_basis(freq_total):
    weights = 1 + np.arange(freq_total) * (NT // 2 // freq_total)
    phase = (weights[:, None] * np.arange(NT)[None, :] % NT) * (2.0 * math.pi / NT)
    scale = 1.0 / math.sqrt(2.0 * freq_total)
    table = np.stack([np.cos(phase) * scale, -np.sin(phase) * scale], axis=1)
    table = table.reshape(2 * freq_total, NT).astype(np.float32)
    high = table.astype(ml_dtypes.bfloat16)
    low = (table - high.astype(np.float32)).astype(ml_dtypes.bfloat16)
    both = np.stack([high, low])
    full = np.zeros((2, 2 * freq_total, GROUP, GROUP, NT), ml_dtypes.bfloat16)
    for g in range(GROUP):
        full[:, :, g, g, :] = both
    return full.reshape(4 * freq_total * GROUP, GROUP * NT)


def shards(tiles, parts, basis, recorded, v_factors, u_factors, tile_ranks, mute_start):
    freqs, _, tile, sources = recorded.shape
    ranks = v_factors.shape[4]
    share = sources // parts
    bf16 = jnp.bfloat16
    spec_shape = (parts, freqs, 2 * tile // parts, sources)
    chunks = tile // parts // (2 * GROUP)
    mask_shape = (chunks, tile * share // chunks, NT)
    anywhere = pl.BlockSpec(memory_space=pl.ANY)
    spectra, mask = pl.pallas_call(
        functools.partial(spectra_kernel, tiles, parts),
        out_shape=(pltpu.VMEM(spec_shape, bf16), pltpu.VMEM(mask_shape, bf16)),
        in_specs=[pl.BlockSpec(memory_space=pltpu.HBM)] * 5,
        out_specs=(pl.BlockSpec(memory_space=pltpu.VMEM),)*2,
        scratch_shapes=[
            pltpu.SMEM(tile_ranks.shape, jnp.int32),
            pltpu.VMEM(recorded.shape, bf16),
            pltpu.VMEM((share, tile), jnp.int32),
            pltpu.VMEM((freqs, tiles, 2 * tile, ranks), bf16),
            pltpu.VMEM((freqs, 2, tile * tiles, ranks), bf16),
            pltpu.VMEM((2, tile * tiles, ranks), jnp.float32),
            pltpu.VMEM((freqs, parts, 2 * share, 2 * tile), bf16),
            pltpu.VMEM((freqs, parts, tiles, share, ranks), bf16),
            pltpu.VMEM((freqs, parts, tiles + 1, share, ranks), bf16),
            pltpu.VMEM((freqs, tile, (tiles + 1) * ranks), bf16),
            pltpu.VMEM((freqs, parts - 1, 2 * tile // parts, sources), bf16),
            pltpu.SemaphoreType.DMA((freqs,)),
            pltpu.SemaphoreType.DMA((freqs,)),
            pltpu.SemaphoreType.DMA((freqs, parts)),
            pltpu.SemaphoreType.DMA((freqs, parts)),
            pltpu.SemaphoreType.DMA((freqs, parts - 1)),
            pltpu.SemaphoreType.DMA((freqs, parts)),
            pltpu.SemaphoreType.DMA((3,)),
        ],
        compiler_params=pltpu.CompilerParams(collective_id=0, has_side_effects=True, vmem_limit_bytes=48 << 20),
        name="spectra_kernel",
    )(
        *[pltpu.with_memory_space_constraint(x, pltpu.HBM) for x in (tile_ranks,
        recorded,
        v_factors.reshape(freqs, tiles, 2 * tile, ranks),
        u_factors.reshape(freqs, 2, tile * tiles, ranks),
        mute_start.T)],
    )
    traces = pl.pallas_call(
        functools.partial(time_kernel, share),
        out_shape=jax.ShapeDtypeStruct((tile * share, NT), jnp.float32),
        in_specs=[pl.BlockSpec(memory_space=pltpu.VMEM)]*3,
        out_specs=pl.BlockSpec(memory_space=pltpu.HBM),
        compiler_params=pltpu.CompilerParams(vmem_limit_bytes=48 << 20),
        scratch_shapes=[
            pltpu.VMEM((tile * share, NT), jnp.float32),
            pltpu.SemaphoreType.DMA((chunks, parts)),
        ],
        name="time_kernel",
    )(spectra, mask, jnp.asarray(basis))
    return traces.reshape(tile, share, NT)


def solution(mesh):
    placed = (
        P("freq", None, "space", None),
        P("freq", None, None, "space", None),
        P("freq", None, "space", None, None),
        P("freq", None, None),
        P("space", "freq"),
    )
    tiles, parts = mesh.shape["space"], mesh.shape["freq"]

    def run(*args):
        body = functools.partial(shards, tiles, parts, block_basis(args[0].shape[0]))
        return jax.shard_map(
            body, mesh=mesh, in_specs=placed, out_specs=P("space", "freq", None), check_vma=False
        )(*args)

    return run
```

```python
import functools
import math

import jax
import jax.numpy as jnp
import ml_dtypes
import numpy as np
from jax import lax
from jax.experimental import pallas as pl
from jax.experimental.pallas import tpu as pltpu
from jax.sharding import PartitionSpec as P

NT = 128
GROUP = 8
LIMIT = 8
NT_DIMS = (((1,), (1,)), ((), ()))


def flipped(index, mask):
    result = index
    bit = 1
    while bit <= mask:
        if mask & bit:
            result = result + bit * (1 - 2 * ((index // bit) % 2))
        bit *= 2
    return result


def crossed(index, other, count):
    result = 0
    bit = 1
    while bit < count:
        here, there = index // bit % 2, other // bit % 2
        result = result + bit * (here + there - 2 * here * there)
        bit *= 2
    return result


def visit_order(parts):
    rows = [list(range(parts - 1, -1, -1))]
    for z in range(1, parts):
        others = [x for x in range(1, parts) if x != z]
        rows.append([0] + sorted(others, key=lambda x: (abs(x - z), x)) + [z])
    return rows


def chosen(rows, index):
    count = len(rows)
    reached = [(index - z + count) // count for z in range(count)] + [0]
    here = [reached[z] - reached[z + 1] for z in range(count)]
    return [sum(rows[z][n] * here[z] for z in range(count)) for n in range(count)]


def spectra_kernel(
    tiles, parts, ranks_hbm, recorded_hbm, v_hbm, u_hbm, mute_hbm, out_ref, mask_ref,
    ranks_ref, recorded_ref, mute_ref, v_ref, u_ref, wide_ref, data_ref, send_ref, recv_ref, factor_ref, spec_ref,
    v_sems, u_sems, send_sems, recv_sems, first_sems, ready_sem,
):
    me = lax.axis_index("space")
    me_z = lax.axis_index("freq")
    freqs = recorded_ref.shape[0]
    tile = recorded_ref.shape[2]
    sources = recorded_ref.shape[3]
    ranks = v_ref.shape[3]
    half = ranks // 2
    share = sources // parts
    rows = tile // parts
    order = list(range(tiles - 1, -1, -1))
    visits = chosen(visit_order(parts), me_z)
    small = tiles <= LIMIT

    v_copies = [
        pltpu.make_async_copy(v_hbm.at[f], v_ref.at[f], v_sems.at[f]) for f in range(freqs)
    ]
    u_copies = [
        pltpu.make_async_copy(u_hbm.at[f], u_ref.at[f], u_sems.at[f]) for f in range(freqs)
    ]
    data_copy = pltpu.make_async_copy(recorded_hbm, recorded_ref, first_sems.at[0])
    ranks_copy = pltpu.make_async_copy(ranks_hbm, ranks_ref, first_sems.at[1])
    mute_copy = pltpu.make_async_copy(mute_hbm, mute_ref, first_sems.at[2])
    data_copy.start()
    v_copies[0].start()
    ranks_copy.start()
    for copy in v_copies[1:] + u_copies:
        copy.start()
    mute_copy.start()

    barrier = pltpu.get_barrier_semaphore()
    for r in range(1, tiles):
        pl.semaphore_signal(
            barrier, inc=1, device_id={"space": flipped(me, r)}, device_id_type=pl.DeviceIdType.MESH
        )
    for r in range(1, parts):
        peer = flipped(me_z, r)

        @pl.when(peer > me_z)
        def _(peer=peer):
            pl.semaphore_signal(
                barrier, inc=1, device_id={"freq": peer}, device_id_type=pl.DeviceIdType.MESH
            )

    def space_copy(f, n, r):
        return pltpu.make_async_remote_copy(
            src_ref=send_ref.at[f, n, r],
            dst_ref=recv_ref.at[f, n, r],
            send_sem=send_sems.at[0],
            recv_sem=recv_sems.at[f, n],
            device_id={"space": flipped(me, r) if small else crossed(me, r, tiles)},
            device_id_type=pl.DeviceIdType.MESH,
        )

    def arrivals(ref, sem):
        return pltpu.make_async_copy(ref.at[pl.ds(1, tiles - 1)], ref.at[pl.ds(1, tiles - 1)], sem)

    def freq_copy(f, n):
        return pltpu.make_async_remote_copy(
            src_ref=spec_ref.at[f, n],
            dst_ref=out_ref.at[me_z, f],
            send_sem=send_sems.at[1],
            recv_sem=send_sems.at[2],
            device_id={"freq": visits[n]},
            device_id_type=pl.DeviceIdType.MESH,
        )

    lane = lax.broadcasted_iota(jnp.int32, (share, ranks), 1)
    low = lane < half
    rank_of = lax.rem(lane, half)
    data_copy.wait()
    for f in range(freqs):
        real = recorded_ref[f, 0].astype(jnp.float32).T.astype(jnp.bfloat16)
        imag = recorded_ref[f, 1].astype(jnp.float32).T.astype(jnp.bfloat16)
        for z in range(parts):
            part = slice(z * share, (z + 1) * share)
            data_ref[f, z, :share, :tile] = real[part]
            data_ref[f, z, :share, tile:] = -imag[part]
            data_ref[f, z, share:, :tile] = -imag[part]
            data_ref[f, z, share:, tile:] = -real[part]
    ranks_copy.wait()

    def send_all(f, steps, low_end, high_end):
        def body(i, _):
            for n in steps:
                space_copy(f, n, i).start()

        lax.fori_loop(low_end, high_end, body, None)

    def first_stage(f, steps):
        lhs = jnp.concatenate([data_ref[f, visits[n]] for n in steps], axis=0)
        for first in range(0, tiles, 2):
            group = order[first : first + 2]
            targets = [flipped(me, r) for r in group]
            pair = jnp.concatenate([v_ref[f, row] for row in targets], axis=1)
            blocks = jnp.dot(lhs, pair, preferred_element_type=jnp.float32)
            for t, (r, row) in enumerate(zip(group, targets)):
                columns = slice(t * ranks, (t + 1) * ranks)
                limit = ranks_ref[f, row, me]
                keep = rank_of < limit
                for i, n in enumerate(steps):
                    at = i * 2 * share
                    real, imag = blocks[at : at + share, columns], blocks[at + share : at + 2 * share, columns]
                    packed = jnp.where(low, real, pltpu.roll(imag, half, 1))
                    packed = jnp.where(keep, packed, 0.0).astype(jnp.bfloat16)
                    if r == 0:
                        recv_ref[f, n, 0] = packed
                        packed = jnp.where(low, pltpu.roll(real, half, 1), imag)
                        kept = rank_of + half < limit
                        recv_ref[f, n, tiles] = jnp.where(kept, packed, 0.0).astype(jnp.bfloat16)
                    else:
                        send_ref[f, n, r] = packed
            done = first + 2
            if not small and done % LIMIT == 0:
                send_all(f, steps, max(tiles - done, 1), tiles - done + LIMIT)

    def send_step(f, n):
        if small:
            for r in order[:-1]:
                space_copy(f, n, r).start()

    def enter():
        pl.semaphore_wait(barrier, tiles - 1 + me_z)
        for r in range(1, parts):
            peer = flipped(me_z, r)

            @pl.when(peer < me_z)
            def _(peer=peer):
                pl.semaphore_signal(
                    ready_sem, inc=1, device_id={"freq": peer}, device_id_type=pl.DeviceIdType.MESH
                )

    if not small:
        enter()

    for f in range(freqs):
        v_copies[f].wait()
        first_stage(f, [0])
        if f == 0 and small:
            enter()
        send_step(f, 0)
    for f in range(freqs):
        first_stage(f, range(1, parts))
        send_step(f, 1)
    for n in range(2, parts):
        for f in range(freqs):
            send_step(f, n)
    wide_low = lax.broadcasted_iota(jnp.int32, (tile, ranks), 1) < half

    def prepare(f):
        u_copies[f].wait()
        for c in range(2):
            wide_ref[c] = u_ref[f, c].astype(jnp.float32)
        for r in range(tiles):
            start = flipped(me, r)
            real = wide_ref[0, pl.ds(start, tile, stride=tiles), :]
            imag = wide_ref[1, pl.ds(start, tile, stride=tiles), :]
            packed = jnp.where(wide_low, real, pltpu.roll(imag, half, 1))
            factor_ref[f, :, r * ranks : (r + 1) * ranks] = packed.astype(jnp.bfloat16)
            if r == 0:
                packed = jnp.where(wide_low, pltpu.roll(real, half, 1), imag)
                factor_ref[f, :, tiles * ranks :] = packed.astype(jnp.bfloat16)

    for f in range(freqs):
        prepare(f)

    mute_copy.wait()
    times = lax.broadcasted_iota(jnp.int32, (share, NT), 1).astype(jnp.float32).astype(jnp.bfloat16)
    one = jnp.ones((share, NT), jnp.bfloat16)
    zero = jnp.zeros((share, NT), jnp.bfloat16)
    span = 2 * GROUP

    def make_masks():
        begins = mute_ref[...].astype(jnp.float32).astype(jnp.bfloat16)
        for n in range(rows // span):
            for q in range(parts):
                for i in range(span):
                    p = q * rows + n * span + i
                    at = (q * span + i) * share
                    mask_ref[n, at : at + share] = jnp.where(times >= begins[:, p : p + 1], one, zero)

    @pl.when(me_z == 0)
    def _():
        make_masks()

    swap_lane = lax.broadcasted_iota(jnp.int32, (rows, sources), 1)
    for n in range(parts):
        for f in range(freqs):
            arrivals(recv_ref.at[f, n], recv_sems.at[f, n]).wait()
            plain, turned = [], []
            for r in range(tiles + 1):
                block = recv_ref[f, n, r]
                plain.append(block)
                swapped = pltpu.roll(block.astype(jnp.float32), half, 1)
                turned.append(jnp.where(low, -swapped, swapped).astype(jnp.bfloat16))
            rhs = jnp.concatenate(
                [jnp.concatenate(plain, axis=1), jnp.concatenate(turned, axis=1)], axis=0
            )
            total = jnp.concatenate(
                [
                    lax.dot_general(factor_ref[f, at : at + tile // 2], rhs, NT_DIMS, preferred_element_type=jnp.float32)
                    for at in (0, tile // 2)
                ],
                axis=0,
            )
            if total.shape[1] < sources:
                total = jnp.concatenate([total, total], axis=1)
            for c in range(2):
                merged = None
                for q in range(parts):
                    piece = total[q * rows : (q + 1) * rows]
                    shift = (q - c) * share % sources
                    if shift:
                        piece = pltpu.roll(piece, shift, 1)
                    merged = piece if q == 0 else jnp.where(swap_lane < q * share, merged, piece)
                merged = merged.astype(jnp.bfloat16)
                if n == parts - 1:
                    out_ref[me_z, f, c * rows : (c + 1) * rows] = merged
                else:
                    spec_ref[f, n, c * rows : (c + 1) * rows] = merged
            if n == 0 and f == 0:
                @pl.when(me_z < parts - 1)
                def _():
                    pl.semaphore_wait(ready_sem, parts - 1 - me_z)

            if n < parts - 1:
                freq_copy(f, n).start()


    @pl.when(me_z > 0)
    def _():
        make_masks()

    everything = send_ref.at[:, :, pl.ds(1, tiles - 1)]
    pltpu.make_async_copy(everything, everything, send_sems.at[0]).wait()
    foreign = spec_ref
    pltpu.make_async_copy(foreign, foreign, send_sems.at[1]).wait()
    foreign = out_ref.at[pl.ds(0, parts - 1)]
    pltpu.make_async_copy(foreign, foreign, send_sems.at[2]).wait()


def time_kernel(
    share, spec_ref, mask_ref, basis_ref, out_hbm, rows_ref, out_sem,
):
    parts, freqs, rows, sources = spec_ref.shape
    rows //= 2
    for n in range(rows // (2 * GROUP)):
        sides = []
        for g in (2 * n, 2 * n + 1):
            pieces = []
            for z in range(parts):
                for f in range(freqs):
                    for c in range(2):
                        at = c * rows + g * GROUP
                        pieces.append(spec_ref[z, f, at : at + GROUP].astype(jnp.float32))
            block = jnp.concatenate(pieces, axis=0)
            sides.append(block.T.astype(jnp.bfloat16))
        lhs = jnp.concatenate(sides, axis=0)
        lhs = jnp.concatenate([lhs, lhs], axis=1)
        for pair in range(GROUP // 2):
            product = jnp.dot(
                lhs, basis_ref[:, pair * 2 * NT : (pair + 1) * 2 * NT], preferred_element_type=jnp.float32
            )
            for side in range(2):
                for q in range(parts):
                    for e in range(2):
                        p = q * rows + (2 * n + side) * GROUP + pair * 2 + e
                        at = side * sources + q * share
                        values = product[at : at + share, e * NT : (e + 1) * NT]
                        row = (q * 2 * GROUP + side * GROUP + pair * 2 + e) * share
                        mask = mask_ref[n, row : row + share].astype(jnp.float32)
                        rows_ref[p * share : (p + 1) * share, :] = values * mask
        for q in range(parts):
            span = pl.ds((q * rows + 2 * n * GROUP) * share, 2 * GROUP * share)
            copy = pltpu.make_async_copy(rows_ref.at[span], out_hbm.at[span], out_sem)
            copy.start()
    pltpu.make_async_copy(rows_ref, out_hbm, out_sem).wait()


def block_basis(freq_total):
    weights = 1 + np.arange(freq_total) * (NT // 2 // freq_total)
    phase = (weights[:, None] * np.arange(NT)[None, :] % NT) * (2.0 * math.pi / NT)
    scale = 1.0 / math.sqrt(2.0 * freq_total)
    table = np.stack([np.cos(phase) * scale, -np.sin(phase) * scale], axis=1)
    table = table.reshape(2 * freq_total, NT).astype(np.float32)
    high = table.astype(ml_dtypes.bfloat16)
    low = (table - high.astype(np.float32)).astype(ml_dtypes.bfloat16)
    both = np.stack([high, low])
    full = np.zeros((2, 2 * freq_total, GROUP, GROUP, NT), ml_dtypes.bfloat16)
    for g in range(GROUP):
        full[:, :, g, g, :] = both
    return full.reshape(4 * freq_total * GROUP, GROUP * NT)


def shards(tiles, parts, basis, recorded, v_factors, u_factors, tile_ranks, mute_start):
    freqs, _, tile, sources = recorded.shape
    ranks = v_factors.shape[4]
    share = sources // parts
    bf16 = jnp.bfloat16
    spec_shape = (parts, freqs, 2 * tile // parts, sources)
    chunks = tile // parts // (2 * GROUP)
    mask_shape = (chunks, tile * share // chunks, NT)
    anywhere = pl.BlockSpec(memory_space=pl.ANY)
    spectra, mask = pl.pallas_call(
        functools.partial(spectra_kernel, tiles, parts),
        out_shape=(pltpu.VMEM(spec_shape, bf16), pltpu.VMEM(mask_shape, bf16)),
        in_specs=[pl.BlockSpec(memory_space=pltpu.HBM)] * 5,
        out_specs=(pl.BlockSpec(memory_space=pltpu.VMEM),)*2,
        scratch_shapes=[
            pltpu.SMEM(tile_ranks.shape, jnp.int32),
            pltpu.VMEM(recorded.shape, bf16),
            pltpu.VMEM((share, tile), jnp.int32),
            pltpu.VMEM((freqs, tiles, 2 * tile, ranks), bf16),
            pltpu.VMEM((freqs, 2, tile * tiles, ranks), bf16),
            pltpu.VMEM((2, tile * tiles, ranks), jnp.float32),
            pltpu.VMEM((freqs, parts, 2 * share, 2 * tile), bf16),
            pltpu.VMEM((freqs, parts, tiles, share, ranks), bf16),
            pltpu.VMEM((freqs, parts, tiles + 1, share, ranks), bf16),
            pltpu.VMEM((freqs, tile, (tiles + 1) * ranks), bf16),
            pltpu.VMEM((freqs, parts - 1, 2 * tile // parts, sources), bf16),
            pltpu.SemaphoreType.DMA((freqs,)),
            pltpu.SemaphoreType.DMA((freqs,)),
            pltpu.SemaphoreType.DMA((3,)),
            pltpu.SemaphoreType.DMA((freqs, parts)),
            pltpu.SemaphoreType.DMA((3,)),
            pltpu.SemaphoreType.REGULAR,
        ],
        compiler_params=pltpu.CompilerParams(collective_id=0, has_side_effects=True, vmem_limit_bytes=48 << 20),
        name="spectra_kernel",
    )(
        *[pltpu.with_memory_space_constraint(x, pltpu.HBM) for x in (tile_ranks,
        recorded,
        v_factors.reshape(freqs, tiles, 2 * tile, ranks),
        u_factors.reshape(freqs, 2, tile * tiles, ranks),
        mute_start.T)],
    )
    traces = pl.pallas_call(
        functools.partial(time_kernel, share),
        out_shape=jax.ShapeDtypeStruct((tile * share, NT), jnp.float32),
        in_specs=[pl.BlockSpec(memory_space=pltpu.VMEM)]*3,
        out_specs=pl.BlockSpec(memory_space=pltpu.HBM),
        compiler_params=pltpu.CompilerParams(vmem_limit_bytes=48 << 20),
        scratch_shapes=[
            pltpu.VMEM((tile * share, NT), jnp.float32),
            pltpu.SemaphoreType.DMA,
        ],
        name="time_kernel",
    )(spectra, mask, jnp.asarray(basis))
    return traces.reshape(tile, share, NT)


def solution(mesh):
    placed = (
        P("freq", None, "space", None),
        P("freq", None, None, "space", None),
        P("freq", None, "space", None, None),
        P("freq", None, None),
        P("space", "freq"),
    )
    tiles, parts = mesh.shape["space"], mesh.shape["freq"]

    def run(*args):
        body = functools.partial(shards, tiles, parts, block_basis(args[0].shape[0]))
        return jax.shard_map(
            body, mesh=mesh, in_specs=placed, out_specs=P("space", "freq", None), check_vma=False
        )(*args)

    return run
```

```python
import functools
import math

import jax
import jax.numpy as jnp
import ml_dtypes
import numpy as np
from jax import lax
from jax.experimental import pallas as pl
from jax.experimental.pallas import tpu as pltpu
from jax.sharding import PartitionSpec as P

NT = 128
GROUP = 8
LIMIT = 8
NT_DIMS = (((1,), (1,)), ((), ()))


def flipped(index, mask):
    result = index
    bit = 1
    while bit <= mask:
        if mask & bit:
            result = result + bit * (1 - 2 * ((index // bit) % 2))
        bit *= 2
    return result


def crossed(index, other, count):
    result = 0
    bit = 1
    while bit < count:
        here, there = index // bit % 2, other // bit % 2
        result = result + bit * (here + there - 2 * here * there)
        bit *= 2
    return result


def visit_order(parts):
    rows = [list(range(parts - 1, -1, -1))]
    for z in range(1, parts):
        others = [x for x in range(1, parts) if x != z]
        rows.append([0] + sorted(others, key=lambda x: (abs(x - z), x)) + [z])
    return rows


def chosen(rows, index):
    count = len(rows)
    reached = [(index - z + count) // count for z in range(count)] + [0]
    here = [reached[z] - reached[z + 1] for z in range(count)]
    return [sum(rows[z][n] * here[z] for z in range(count)) for n in range(count)]


def spectra_kernel(
    tiles, parts, ranks_hbm, recorded_hbm, v_hbm, u_hbm, mute_hbm, out_ref, mask_ref,
    ranks_ref, recorded_ref, mute_ref, v_ref, u_ref, wide_ref, data_ref, send_ref, recv_ref, factor_ref, spec_ref,
    v_sems, u_sems, send_sems, recv_sems, first_sems, ready_sem,
):
    me = lax.axis_index("space")
    me_z = lax.axis_index("freq")
    freqs = recorded_ref.shape[0]
    tile = recorded_ref.shape[2]
    sources = recorded_ref.shape[3]
    ranks = v_ref.shape[3]
    half = ranks // 2
    share = sources // parts
    rows = tile // parts
    order = list(range(tiles - 1, -1, -1))
    same_core_first = sorted(range(1, tiles), key=lambda r: (-(r // 2), r % 2))
    visits = chosen(visit_order(parts), me_z)
    small = tiles <= LIMIT

    v_copies = [
        pltpu.make_async_copy(v_hbm.at[f], v_ref.at[f], v_sems.at[f]) for f in range(freqs)
    ]
    u_copies = [
        pltpu.make_async_copy(u_hbm.at[f], u_ref.at[f], u_sems.at[f]) for f in range(freqs)
    ]
    data_copy = pltpu.make_async_copy(recorded_hbm, recorded_ref, first_sems.at[0])
    ranks_copy = pltpu.make_async_copy(ranks_hbm, ranks_ref, first_sems.at[1])
    mute_copy = pltpu.make_async_copy(mute_hbm, mute_ref, first_sems.at[2])
    data_copy.start()
    v_copies[0].start()
    ranks_copy.start()
    for copy in v_copies[1:] + u_copies:
        copy.start()
    mute_copy.start()

    barrier = pltpu.get_barrier_semaphore()
    for r in range(1, tiles):
        pl.semaphore_signal(
            barrier, inc=1, device_id={"space": flipped(me, r)}, device_id_type=pl.DeviceIdType.MESH
        )
    for r in range(1, parts):
        peer = flipped(me_z, r)

        @pl.when(peer > me_z)
        def _(peer=peer):
            pl.semaphore_signal(
                barrier, inc=1, device_id={"freq": peer}, device_id_type=pl.DeviceIdType.MESH
            )

    def space_copy(f, n, r):
        return pltpu.make_async_remote_copy(
            src_ref=send_ref.at[f, n, r],
            dst_ref=recv_ref.at[f, n, r],
            send_sem=send_sems.at[0],
            recv_sem=recv_sems.at[f, n],
            device_id={"space": flipped(me, r) if small else crossed(me, r, tiles)},
            device_id_type=pl.DeviceIdType.MESH,
        )

    def arrivals(ref, sem):
        return pltpu.make_async_copy(ref.at[pl.ds(1, tiles - 1)], ref.at[pl.ds(1, tiles - 1)], sem)

    def freq_copy(f, n):
        return pltpu.make_async_remote_copy(
            src_ref=spec_ref.at[f, n],
            dst_ref=out_ref.at[me_z, f],
            send_sem=send_sems.at[1],
            recv_sem=send_sems.at[2],
            device_id={"freq": visits[n]},
            device_id_type=pl.DeviceIdType.MESH,
        )

    lane = lax.broadcasted_iota(jnp.int32, (share, ranks), 1)
    low = lane < half
    rank_of = lax.rem(lane, half)
    data_copy.wait()
    for f in range(freqs):
        real = recorded_ref[f, 0].astype(jnp.float32).T.astype(jnp.bfloat16)
        imag = recorded_ref[f, 1].astype(jnp.float32).T.astype(jnp.bfloat16)
        for z in range(parts):
            part = slice(z * share, (z + 1) * share)
            data_ref[f, z, :share, :tile] = real[part]
            data_ref[f, z, :share, tile:] = -imag[part]
            data_ref[f, z, share:, :tile] = -imag[part]
            data_ref[f, z, share:, tile:] = -real[part]
    ranks_copy.wait()

    def send_all(f, steps, low_end, high_end):
        def body(i, _):
            for n in steps:
                space_copy(f, n, i).start()

        lax.fori_loop(low_end, high_end, body, None)

    def first_stage(f, steps):
        lhs = jnp.concatenate([data_ref[f, visits[n]] for n in steps], axis=0)
        for first in range(0, tiles, 2):
            group = order[first : first + 2]
            targets = [flipped(me, r) for r in group]
            pair = jnp.concatenate([v_ref[f, row] for row in targets], axis=1)
            blocks = jnp.dot(lhs, pair, preferred_element_type=jnp.float32)
            for t, (r, row) in enumerate(zip(group, targets)):
                columns = slice(t * ranks, (t + 1) * ranks)
                limit = ranks_ref[f, row, me]
                keep = rank_of < limit
                for i, n in enumerate(steps):
                    at = i * 2 * share
                    real, imag = blocks[at : at + share, columns], blocks[at + share : at + 2 * share, columns]
                    packed = jnp.where(low, real, pltpu.roll(imag, half, 1))
                    packed = jnp.where(keep, packed, 0.0).astype(jnp.bfloat16)
                    if r == 0:
                        recv_ref[f, n, 0] = packed
                        packed = jnp.where(low, pltpu.roll(real, half, 1), imag)
                        kept = rank_of + half < limit
                        recv_ref[f, n, tiles] = jnp.where(kept, packed, 0.0).astype(jnp.bfloat16)
                    else:
                        send_ref[f, n, r] = packed
            done = first + 2
            if not small and done % LIMIT == 0:
                send_all(f, steps, max(tiles - done, 1), tiles - done + LIMIT)

    def send_step(f, n):
        if small:
            for r in order[:-1] if n == 0 else same_core_first:
                space_copy(f, n, r).start()

    def enter():
        pl.semaphore_wait(barrier, tiles - 1 + me_z)
        for r in range(1, parts):
            peer = flipped(me_z, r)

            @pl.when(peer < me_z)
            def _(peer=peer):
                pl.semaphore_signal(
                    ready_sem, inc=1, device_id={"freq": peer}, device_id_type=pl.DeviceIdType.MESH
                )

    if not small:
        enter()

    for f in range(freqs):
        v_copies[f].wait()
        first_stage(f, [0])
        if f == 0 and small:
            enter()
        send_step(f, 0)
    for f in range(freqs):
        first_stage(f, range(1, parts))
        send_step(f, 1)
    for n in range(2, parts):
        for f in range(freqs):
            send_step(f, n)
    wide_low = lax.broadcasted_iota(jnp.int32, (tile, ranks), 1) < half

    def prepare(f):
        u_copies[f].wait()
        for c in range(2):
            wide_ref[c] = u_ref[f, c].astype(jnp.float32)
        for r in range(tiles):
            start = flipped(me, r)
            real = wide_ref[0, pl.ds(start, tile, stride=tiles), :]
            imag = wide_ref[1, pl.ds(start, tile, stride=tiles), :]
            packed = jnp.where(wide_low, real, pltpu.roll(imag, half, 1))
            factor_ref[f, :, r * ranks : (r + 1) * ranks] = packed.astype(jnp.bfloat16)
            if r == 0:
                packed = jnp.where(wide_low, pltpu.roll(real, half, 1), imag)
                factor_ref[f, :, tiles * ranks :] = packed.astype(jnp.bfloat16)

    for f in range(freqs):
        prepare(f)

    mute_copy.wait()
    times = lax.broadcasted_iota(jnp.int32, (share, NT), 1).astype(jnp.float32).astype(jnp.bfloat16)
    one = jnp.ones((share, NT), jnp.bfloat16)
    zero = jnp.zeros((share, NT), jnp.bfloat16)
    span = 2 * GROUP

    def make_masks():
        begins = mute_ref[...].astype(jnp.float32).astype(jnp.bfloat16)
        for n in range(rows // span):
            for q in range(parts):
                for i in range(span):
                    p = q * rows + n * span + i
                    at = (q * span + i) * share
                    mask_ref[n, at : at + share] = jnp.where(times >= begins[:, p : p + 1], one, zero)

    @pl.when(me_z == 0)
    def _():
        make_masks()

    swap_lane = lax.broadcasted_iota(jnp.int32, (rows, sources), 1)
    for n in range(parts):
        for f in range(freqs):
            arrivals(recv_ref.at[f, n], recv_sems.at[f, n]).wait()
            plain, turned = [], []
            for r in range(tiles + 1):
                block = recv_ref[f, n, r]
                plain.append(block)
                swapped = pltpu.roll(block.astype(jnp.float32), half, 1)
                turned.append(jnp.where(low, -swapped, swapped).astype(jnp.bfloat16))
            rhs = jnp.concatenate(
                [jnp.concatenate(plain, axis=1), jnp.concatenate(turned, axis=1)], axis=0
            )
            total = jnp.concatenate(
                [
                    lax.dot_general(factor_ref[f, at : at + tile // 2], rhs, NT_DIMS, preferred_element_type=jnp.float32)
                    for at in (0, tile // 2)
                ],
                axis=0,
            )
            if total.shape[1] < sources:
                total = jnp.concatenate([total, total], axis=1)
            for c in range(2):
                merged = None
                for q in range(parts):
                    piece = total[q * rows : (q + 1) * rows]
                    shift = (q - c) * share % sources
                    if shift:
                        piece = pltpu.roll(piece, shift, 1)
                    merged = piece if q == 0 else jnp.where(swap_lane < q * share, merged, piece)
                merged = merged.astype(jnp.bfloat16)
                if n == parts - 1:
                    out_ref[me_z, f, c * rows : (c + 1) * rows] = merged
                else:
                    spec_ref[f, n, c * rows : (c + 1) * rows] = merged
            if n == 0 and f == 0:
                @pl.when(me_z < parts - 1)
                def _():
                    pl.semaphore_wait(ready_sem, parts - 1 - me_z)

            if n < parts - 1:
                freq_copy(f, n).start()


    @pl.when(me_z > 0)
    def _():
        make_masks()

    everything = send_ref.at[:, :, pl.ds(1, tiles - 1)]
    pltpu.make_async_copy(everything, everything, send_sems.at[0]).wait()
    foreign = spec_ref
    pltpu.make_async_copy(foreign, foreign, send_sems.at[1]).wait()
    foreign = out_ref.at[pl.ds(0, parts - 1)]
    pltpu.make_async_copy(foreign, foreign, send_sems.at[2]).wait()


def time_kernel(
    share, spec_ref, mask_ref, basis_ref, out_hbm, rows_ref, out_sem,
):
    parts, freqs, rows, sources = spec_ref.shape
    rows //= 2
    for n in range(rows // (2 * GROUP)):
        sides = []
        for g in (2 * n, 2 * n + 1):
            pieces = []
            for z in range(parts):
                for f in range(freqs):
                    for c in range(2):
                        at = c * rows + g * GROUP
                        pieces.append(spec_ref[z, f, at : at + GROUP].astype(jnp.float32))
            block = jnp.concatenate(pieces, axis=0)
            sides.append(block.T.astype(jnp.bfloat16))
        lhs = jnp.concatenate(sides, axis=0)
        lhs = jnp.concatenate([lhs, lhs], axis=1)
        for pair in range(GROUP // 2):
            product = jnp.dot(
                lhs, basis_ref[:, pair * 2 * NT : (pair + 1) * 2 * NT], preferred_element_type=jnp.float32
            )
            for side in range(2):
                for q in range(parts):
                    for e in range(2):
                        p = q * rows + (2 * n + side) * GROUP + pair * 2 + e
                        at = side * sources + q * share
                        values = product[at : at + share, e * NT : (e + 1) * NT]
                        row = (q * 2 * GROUP + side * GROUP + pair * 2 + e) * share
                        mask = mask_ref[n, row : row + share].astype(jnp.float32)
                        rows_ref[p * share : (p + 1) * share, :] = values * mask
        for q in range(parts):
            span = pl.ds((q * rows + 2 * n * GROUP) * share, 2 * GROUP * share)
            copy = pltpu.make_async_copy(rows_ref.at[span], out_hbm.at[span], out_sem)
            copy.start()
    pltpu.make_async_copy(rows_ref, out_hbm, out_sem).wait()


def block_basis(freq_total):
    weights = 1 + np.arange(freq_total) * (NT // 2 // freq_total)
    phase = (weights[:, None] * np.arange(NT)[None, :] % NT) * (2.0 * math.pi / NT)
    scale = 1.0 / math.sqrt(2.0 * freq_total)
    table = np.stack([np.cos(phase) * scale, -np.sin(phase) * scale], axis=1)
    table = table.reshape(2 * freq_total, NT).astype(np.float32)
    high = table.astype(ml_dtypes.bfloat16)
    low = (table - high.astype(np.float32)).astype(ml_dtypes.bfloat16)
    both = np.stack([high, low])
    full = np.zeros((2, 2 * freq_total, GROUP, GROUP, NT), ml_dtypes.bfloat16)
    for g in range(GROUP):
        full[:, :, g, g, :] = both
    return full.reshape(4 * freq_total * GROUP, GROUP * NT)


def shards(tiles, parts, basis, recorded, v_factors, u_factors, tile_ranks, mute_start):
    freqs, _, tile, sources = recorded.shape
    ranks = v_factors.shape[4]
    share = sources // parts
    bf16 = jnp.bfloat16
    spec_shape = (parts, freqs, 2 * tile // parts, sources)
    chunks = tile // parts // (2 * GROUP)
    mask_shape = (chunks, tile * share // chunks, NT)
    anywhere = pl.BlockSpec(memory_space=pl.ANY)
    spectra, mask = pl.pallas_call(
        functools.partial(spectra_kernel, tiles, parts),
        out_shape=(pltpu.VMEM(spec_shape, bf16), pltpu.VMEM(mask_shape, bf16)),
        in_specs=[pl.BlockSpec(memory_space=pltpu.HBM)] * 5,
        out_specs=(pl.BlockSpec(memory_space=pltpu.VMEM),)*2,
        scratch_shapes=[
            pltpu.SMEM(tile_ranks.shape, jnp.int32),
            pltpu.VMEM(recorded.shape, bf16),
            pltpu.VMEM((share, tile), jnp.int32),
            pltpu.VMEM((freqs, tiles, 2 * tile, ranks), bf16),
            pltpu.VMEM((freqs, 2, tile * tiles, ranks), bf16),
            pltpu.VMEM((2, tile * tiles, ranks), jnp.float32),
            pltpu.VMEM((freqs, parts, 2 * share, 2 * tile), bf16),
            pltpu.VMEM((freqs, parts, tiles, share, ranks), bf16),
            pltpu.VMEM((freqs, parts, tiles + 1, share, ranks), bf16),
            pltpu.VMEM((freqs, tile, (tiles + 1) * ranks), bf16),
            pltpu.VMEM((freqs, parts - 1, 2 * tile // parts, sources), bf16),
            pltpu.SemaphoreType.DMA((freqs,)),
            pltpu.SemaphoreType.DMA((freqs,)),
            pltpu.SemaphoreType.DMA((3,)),
            pltpu.SemaphoreType.DMA((freqs, parts)),
            pltpu.SemaphoreType.DMA((3,)),
            pltpu.SemaphoreType.REGULAR,
        ],
        compiler_params=pltpu.CompilerParams(collective_id=0, has_side_effects=True, vmem_limit_bytes=48 << 20),
        name="spectra_kernel",
    )(
        *[pltpu.with_memory_space_constraint(x, pltpu.HBM) for x in (tile_ranks,
        recorded,
        v_factors.reshape(freqs, tiles, 2 * tile, ranks),
        u_factors.reshape(freqs, 2, tile * tiles, ranks),
        mute_start.T)],
    )
    traces = pl.pallas_call(
        functools.partial(time_kernel, share),
        out_shape=jax.ShapeDtypeStruct((tile * share, NT), jnp.float32),
        in_specs=[pl.BlockSpec(memory_space=pltpu.VMEM)]*3,
        out_specs=pl.BlockSpec(memory_space=pltpu.HBM),
        compiler_params=pltpu.CompilerParams(vmem_limit_bytes=48 << 20),
        scratch_shapes=[
            pltpu.VMEM((tile * share, NT), jnp.float32),
            pltpu.SemaphoreType.DMA,
        ],
        name="time_kernel",
    )(spectra, mask, jnp.asarray(basis))
    return traces.reshape(tile, share, NT)


def solution(mesh):
    placed = (
        P("freq", None, "space", None),
        P("freq", None, None, "space", None),
        P("freq", None, "space", None, None),
        P("freq", None, None),
        P("space", "freq"),
    )
    tiles, parts = mesh.shape["space"], mesh.shape["freq"]

    def run(*args):
        body = functools.partial(shards, tiles, parts, block_basis(args[0].shape[0]))
        return jax.shard_map(
            body, mesh=mesh, in_specs=placed, out_specs=P("space", "freq", None), check_vma=False
        )(*args)

    return run
```

```python
import functools
import math

import jax
import jax.numpy as jnp
import ml_dtypes
import numpy as np
from jax import lax
from jax.experimental import pallas as pl
from jax.experimental.pallas import tpu as pltpu
from jax.sharding import PartitionSpec as P

NT = 128
GROUP = 8
LIMIT = 8
NT_DIMS = (((1,), (1,)), ((), ()))


def flipped(index, mask):
    result = index
    bit = 1
    while bit <= mask:
        if mask & bit:
            result = result + bit * (1 - 2 * ((index // bit) % 2))
        bit *= 2
    return result


def crossed(index, other, count):
    result = 0
    bit = 1
    while bit < count:
        here, there = index // bit % 2, other // bit % 2
        result = result + bit * (here + there - 2 * here * there)
        bit *= 2
    return result


def visit_order(parts):
    rows = [list(range(parts - 1, -1, -1))]
    for z in range(1, parts):
        others = [x for x in range(1, parts) if x != z]
        rows.append([0] + sorted(others, key=lambda x: (abs(x - z), x)) + [z])
    return rows


def chosen(rows, index):
    count = len(rows)
    reached = [(index - z + count) // count for z in range(count)] + [0]
    here = [reached[z] - reached[z + 1] for z in range(count)]
    return [sum(rows[z][n] * here[z] for z in range(count)) for n in range(count)]


def spectra_kernel(
    tiles, parts, ranks_hbm, recorded_hbm, v_hbm, u_hbm, mute_hbm, out_ref, mask_ref,
    ranks_ref, recorded_ref, mute_ref, v_ref, u_ref, wide_ref, data_ref, send_ref, recv_ref, factor_ref, spec_ref,
    v_sems, u_sems, send_sems, recv_sems, first_sems, ready_sem,
):
    me = lax.axis_index("space")
    me_z = lax.axis_index("freq")
    freqs = recorded_ref.shape[0]
    tile = recorded_ref.shape[2]
    sources = recorded_ref.shape[3]
    ranks = v_ref.shape[3]
    half = ranks // 2
    share = sources // parts
    rows = tile // parts
    order = list(range(tiles - 1, -1, -1))
    same_core_first = sorted(range(1, tiles), key=lambda r: (-(r // 2), r % 2))
    visits = chosen(visit_order(parts), me_z)
    small = tiles <= LIMIT

    v_copies = [
        pltpu.make_async_copy(v_hbm.at[f], v_ref.at[f], v_sems.at[f]) for f in range(freqs)
    ]
    u_copies = [
        pltpu.make_async_copy(u_hbm.at[f], u_ref.at[f], u_sems.at[f]) for f in range(freqs)
    ]
    data_copy = pltpu.make_async_copy(recorded_hbm, recorded_ref, first_sems.at[0])
    ranks_copy = pltpu.make_async_copy(ranks_hbm, ranks_ref, first_sems.at[1])
    mute_copy = pltpu.make_async_copy(mute_hbm, mute_ref, first_sems.at[2])
    data_copy.start()
    v_copies[0].start()
    ranks_copy.start()
    for copy in v_copies[1:] + u_copies:
        copy.start()
    mute_copy.start()

    barrier = pltpu.get_barrier_semaphore()
    for r in range(1, tiles):
        pl.semaphore_signal(
            barrier, inc=1, device_id={"space": flipped(me, r)}, device_id_type=pl.DeviceIdType.MESH
        )
    for r in range(1, parts):
        peer = flipped(me_z, r)

        @pl.when(peer > me_z)
        def _(peer=peer):
            pl.semaphore_signal(
                barrier, inc=1, device_id={"freq": peer}, device_id_type=pl.DeviceIdType.MESH
            )

    def space_copy(f, n, r):
        return pltpu.make_async_remote_copy(
            src_ref=send_ref.at[f, n, r],
            dst_ref=recv_ref.at[f, n, r],
            send_sem=send_sems.at[0],
            recv_sem=recv_sems.at[f, n],
            device_id={"space": flipped(me, r) if small else crossed(me, r, tiles)},
            device_id_type=pl.DeviceIdType.MESH,
        )

    def arrivals(ref, sem):
        return pltpu.make_async_copy(ref.at[pl.ds(1, tiles - 1)], ref.at[pl.ds(1, tiles - 1)], sem)

    def freq_copy(f, n):
        return pltpu.make_async_remote_copy(
            src_ref=spec_ref.at[f, n],
            dst_ref=out_ref.at[me_z, f],
            send_sem=send_sems.at[1],
            recv_sem=send_sems.at[2],
            device_id={"freq": visits[n]},
            device_id_type=pl.DeviceIdType.MESH,
        )

    lane = lax.broadcasted_iota(jnp.int32, (share, ranks), 1)
    low = lane < half
    rank_of = lax.rem(lane, half)
    data_copy.wait()
    for f in range(freqs):
        real = recorded_ref[f, 0].astype(jnp.float32).T.astype(jnp.bfloat16)
        imag = recorded_ref[f, 1].astype(jnp.float32).T.astype(jnp.bfloat16)
        for z in range(parts):
            part = slice(z * share, (z + 1) * share)
            data_ref[f, z, :share, :tile] = real[part]
            data_ref[f, z, :share, tile:] = -imag[part]
            data_ref[f, z, share:, :tile] = -imag[part]
            data_ref[f, z, share:, tile:] = -real[part]
    ranks_copy.wait()

    def send_all(f, steps, low_end, high_end):
        def body(i, _):
            for n in steps:
                space_copy(f, n, i).start()

        lax.fori_loop(low_end, high_end, body, None)

    def first_stage(f, steps):
        lhs = jnp.concatenate([data_ref[f, visits[n]] for n in steps], axis=0)
        for first in range(0, tiles, 2):
            group = order[first : first + 2]
            targets = [flipped(me, r) for r in group]
            pair = jnp.concatenate([v_ref[f, row] for row in targets], axis=1)
            blocks = jnp.dot(lhs, pair, preferred_element_type=jnp.float32)
            for t, (r, row) in enumerate(zip(group, targets)):
                columns = slice(t * ranks, (t + 1) * ranks)
                limit = ranks_ref[f, row, me]
                keep = rank_of < limit
                for i, n in enumerate(steps):
                    at = i * 2 * share
                    real, imag = blocks[at : at + share, columns], blocks[at + share : at + 2 * share, columns]
                    packed = jnp.where(low, real, pltpu.roll(imag, half, 1))
                    packed = jnp.where(keep, packed, 0.0).astype(jnp.bfloat16)
                    if r == 0:
                        recv_ref[f, n, 0] = packed
                        packed = jnp.where(low, pltpu.roll(real, half, 1), imag)
                        kept = rank_of + half < limit
                        recv_ref[f, n, tiles] = jnp.where(kept, packed, 0.0).astype(jnp.bfloat16)
                    else:
                        send_ref[f, n, r] = packed
            done = first + 2
            if not small and done % LIMIT == 0:
                send_all(f, steps, max(tiles - done, 1), tiles - done + LIMIT)

    def send_step(f, n):
        if small:
            for r in order[:-1] if n == 0 else same_core_first:
                space_copy(f, n, r).start()

    def enter():
        pl.semaphore_wait(barrier, tiles - 1 + me_z)
        for r in range(1, parts):
            peer = flipped(me_z, r)

            @pl.when(peer < me_z)
            def _(peer=peer):
                pl.semaphore_signal(
                    ready_sem, inc=1, device_id={"freq": peer}, device_id_type=pl.DeviceIdType.MESH
                )

    if not small:
        enter()

    for f in range(freqs):
        v_copies[f].wait()
        first_stage(f, [0])
        if f == 0 and small:
            enter()
        send_step(f, 0)
    for f in range(freqs):
        first_stage(f, range(1, parts))
        send_step(f, 1)
    for n in range(2, parts):
        for f in range(freqs):
            send_step(f, n)
    wide_low = lax.broadcasted_iota(jnp.int32, (tile, ranks), 1) < half

    def prepare(f):
        u_copies[f].wait()
        for c in range(2):
            wide_ref[c] = u_ref[f, c].astype(jnp.float32)
        for r in range(tiles):
            start = flipped(me, r)
            real = wide_ref[0, pl.ds(start, tile, stride=tiles), :]
            imag = wide_ref[1, pl.ds(start, tile, stride=tiles), :]
            packed = jnp.where(wide_low, real, pltpu.roll(imag, half, 1))
            factor_ref[f, :, r * ranks : (r + 1) * ranks] = packed.astype(jnp.bfloat16)
            if r == 0:
                packed = jnp.where(wide_low, pltpu.roll(real, half, 1), imag)
                factor_ref[f, :, tiles * ranks :] = packed.astype(jnp.bfloat16)

    for f in range(freqs):
        prepare(f)

    mute_copy.wait()
    times = lax.broadcasted_iota(jnp.int32, (share, NT), 1).astype(jnp.float32).astype(jnp.bfloat16)
    one = jnp.ones((share, NT), jnp.bfloat16)
    zero = jnp.zeros((share, NT), jnp.bfloat16)
    span = 2 * GROUP

    def make_masks():
        begins = mute_ref[...].astype(jnp.float32).astype(jnp.bfloat16)
        for n in range(rows // span):
            for q in range(parts):
                for i in range(span):
                    p = q * rows + n * span + i
                    at = (q * span + i) * share
                    mask_ref[n, at : at + share] = jnp.where(times >= begins[:, p : p + 1], one, zero)

    @pl.when(me_z == 0)
    def _():
        make_masks()

    swap_lane = lax.broadcasted_iota(jnp.int32, (rows, sources), 1)
    for n in range(parts):
        for f in range(freqs):
            def product(blocks, splits):
                plain, turned = [], []
                for r in blocks:
                    block = recv_ref[f, n, r]
                    plain.append(block)
                    swapped = pltpu.roll(block.astype(jnp.float32), half, 1)
                    turned.append(jnp.where(low, -swapped, swapped).astype(jnp.bfloat16))
                rhs = jnp.concatenate(
                    [jnp.concatenate(plain, axis=1), jnp.concatenate(turned, axis=1)], axis=0
                )
                sides = []
                for i in range(splits):
                    span = pl.ds(i * tile // splits, tile // splits)
                    lhs = jnp.concatenate(
                        [factor_ref[f, span, r * ranks : (r + 1) * ranks] for r in blocks], axis=1
                    )
                    sides.append(lax.dot_general(lhs, rhs, NT_DIMS, preferred_element_type=jnp.float32))
                return jnp.concatenate(sides, axis=0)

            early = product((0, tiles), 2) if n == 0 and f == 0 else None
            arrivals(recv_ref.at[f, n], recv_sems.at[f, n]).wait()
            total = product(range(tiles + 1), 2) if early is None else product(range(1, tiles), 2) + early
            if total.shape[1] < sources:
                total = jnp.concatenate([total, total], axis=1)
            for c in range(2):
                merged = None
                for q in range(parts):
                    piece = total[q * rows : (q + 1) * rows]
                    shift = (q - c) * share % sources
                    if shift:
                        piece = pltpu.roll(piece, shift, 1)
                    merged = piece if q == 0 else jnp.where(swap_lane < q * share, merged, piece)
                merged = merged.astype(jnp.bfloat16)
                if n == parts - 1:
                    out_ref[me_z, f, c * rows : (c + 1) * rows] = merged
                else:
                    spec_ref[f, n, c * rows : (c + 1) * rows] = merged
            if n == 0 and f == 0:
                @pl.when(me_z < parts - 1)
                def _():
                    pl.semaphore_wait(ready_sem, parts - 1 - me_z)

            if n < parts - 1:
                freq_copy(f, n).start()


    @pl.when(me_z > 0)
    def _():
        make_masks()

    everything = send_ref.at[:, :, pl.ds(1, tiles - 1)]
    pltpu.make_async_copy(everything, everything, send_sems.at[0]).wait()
    foreign = spec_ref
    pltpu.make_async_copy(foreign, foreign, send_sems.at[1]).wait()
    foreign = out_ref.at[pl.ds(0, parts - 1)]
    pltpu.make_async_copy(foreign, foreign, send_sems.at[2]).wait()


def time_kernel(
    share, spec_ref, mask_ref, basis_ref, out_hbm, rows_ref, out_sem,
):
    parts, freqs, rows, sources = spec_ref.shape
    rows //= 2
    chunks = [(0, (0,)), (0, (1,))] + [(n, (0, 1)) for n in range(1, rows // (2 * GROUP))]
    for n, chosen_sides in chunks:
        sides = []
        for side in chosen_sides:
            g = 2 * n + side
            pieces = []
            for z in range(parts):
                for f in range(freqs):
                    for c in range(2):
                        at = c * rows + g * GROUP
                        pieces.append(spec_ref[z, f, at : at + GROUP].astype(jnp.float32))
            block = jnp.concatenate(pieces, axis=0)
            sides.append(block.T.astype(jnp.bfloat16))
        lhs = jnp.concatenate(sides, axis=0)
        lhs = jnp.concatenate([lhs, lhs], axis=1)
        for pair in range(GROUP // 2):
            product = jnp.dot(
                lhs, basis_ref[:, pair * 2 * NT : (pair + 1) * 2 * NT], preferred_element_type=jnp.float32
            )
            for i, side in enumerate(chosen_sides):
                for q in range(parts):
                    for e in range(2):
                        p = q * rows + (2 * n + side) * GROUP + pair * 2 + e
                        at = i * sources + q * share
                        values = product[at : at + share, e * NT : (e + 1) * NT]
                        row = (q * 2 * GROUP + side * GROUP + pair * 2 + e) * share
                        mask = mask_ref[n, row : row + share].astype(jnp.float32)
                        rows_ref[p * share : (p + 1) * share, :] = values * mask
        count = len(chosen_sides) * GROUP * share
        for q in range(parts):
            span = pl.ds((q * rows + (2 * n + chosen_sides[0]) * GROUP) * share, count)
            pltpu.make_async_copy(rows_ref.at[span], out_hbm.at[span], out_sem).start()
    pltpu.make_async_copy(rows_ref, out_hbm, out_sem).wait()


def block_basis(freq_total):
    weights = 1 + np.arange(freq_total) * (NT // 2 // freq_total)
    phase = (weights[:, None] * np.arange(NT)[None, :] % NT) * (2.0 * math.pi / NT)
    scale = 1.0 / math.sqrt(2.0 * freq_total)
    table = np.stack([np.cos(phase) * scale, -np.sin(phase) * scale], axis=1)
    table = table.reshape(2 * freq_total, NT).astype(np.float32)
    high = table.astype(ml_dtypes.bfloat16)
    low = (table - high.astype(np.float32)).astype(ml_dtypes.bfloat16)
    both = np.stack([high, low])
    full = np.zeros((2, 2 * freq_total, GROUP, GROUP, NT), ml_dtypes.bfloat16)
    for g in range(GROUP):
        full[:, :, g, g, :] = both
    return full.reshape(4 * freq_total * GROUP, GROUP * NT)


def shards(tiles, parts, basis, recorded, v_factors, u_factors, tile_ranks, mute_start):
    freqs, _, tile, sources = recorded.shape
    ranks = v_factors.shape[4]
    share = sources // parts
    bf16 = jnp.bfloat16
    spec_shape = (parts, freqs, 2 * tile // parts, sources)
    chunks = tile // parts // (2 * GROUP)
    mask_shape = (chunks, tile * share // chunks, NT)
    anywhere = pl.BlockSpec(memory_space=pl.ANY)
    spectra, mask = pl.pallas_call(
        functools.partial(spectra_kernel, tiles, parts),
        out_shape=(pltpu.VMEM(spec_shape, bf16), pltpu.VMEM(mask_shape, bf16)),
        in_specs=[pl.BlockSpec(memory_space=pltpu.HBM)] * 5,
        out_specs=(pl.BlockSpec(memory_space=pltpu.VMEM),)*2,
        scratch_shapes=[
            pltpu.SMEM(tile_ranks.shape, jnp.int32),
            pltpu.VMEM(recorded.shape, bf16),
            pltpu.VMEM((share, tile), jnp.int32),
            pltpu.VMEM((freqs, tiles, 2 * tile, ranks), bf16),
            pltpu.VMEM((freqs, 2, tile * tiles, ranks), bf16),
            pltpu.VMEM((2, tile * tiles, ranks), jnp.float32),
            pltpu.VMEM((freqs, parts, 2 * share, 2 * tile), bf16),
            pltpu.VMEM((freqs, parts, tiles, share, ranks), bf16),
            pltpu.VMEM((freqs, parts, tiles + 1, share, ranks), bf16),
            pltpu.VMEM((freqs, tile, (tiles + 1) * ranks), bf16),
            pltpu.VMEM((freqs, parts - 1, 2 * tile // parts, sources), bf16),
            pltpu.SemaphoreType.DMA((freqs,)),
            pltpu.SemaphoreType.DMA((freqs,)),
            pltpu.SemaphoreType.DMA((3,)),
            pltpu.SemaphoreType.DMA((freqs, parts)),
            pltpu.SemaphoreType.DMA((3,)),
            pltpu.SemaphoreType.REGULAR,
        ],
        compiler_params=pltpu.CompilerParams(collective_id=0, has_side_effects=True, vmem_limit_bytes=48 << 20),
        name="spectra_kernel",
    )(
        *[pltpu.with_memory_space_constraint(x, pltpu.HBM) for x in (tile_ranks,
        recorded,
        v_factors.reshape(freqs, tiles, 2 * tile, ranks),
        u_factors.reshape(freqs, 2, tile * tiles, ranks),
        mute_start.T)],
    )
    traces = pl.pallas_call(
        functools.partial(time_kernel, share),
        out_shape=jax.ShapeDtypeStruct((tile * share, NT), jnp.float32),
        in_specs=[pl.BlockSpec(memory_space=pltpu.VMEM)]*3,
        out_specs=pl.BlockSpec(memory_space=pltpu.HBM),
        compiler_params=pltpu.CompilerParams(vmem_limit_bytes=48 << 20),
        scratch_shapes=[
            pltpu.VMEM((tile * share, NT), jnp.float32),
            pltpu.SemaphoreType.DMA,
        ],
        name="time_kernel",
    )(spectra, mask, jnp.asarray(basis))
    return traces.reshape(tile, share, NT)


def solution(mesh):
    placed = (
        P("freq", None, "space", None),
        P("freq", None, None, "space", None),
        P("freq", None, "space", None, None),
        P("freq", None, None),
        P("space", "freq"),
    )
    tiles, parts = mesh.shape["space"], mesh.shape["freq"]

    def run(*args):
        body = functools.partial(shards, tiles, parts, block_basis(args[0].shape[0]))
        return jax.shard_map(
            body, mesh=mesh, in_specs=placed, out_specs=P("space", "freq", None), check_vma=False
        )(*args)

    return run
```
